256 devices in a mesh: dp: 32 (over z, x), tensor: 8 (over y, core).
Axes of the slice: x: 4, y: 4, z: 8, core: 2. Of those that a mesh axis runs over, the one named last changes fastest.
Arguments:
- layer_input: bfloat16 [65536, 5120], P('dp', 'tensor'), may hold values from -6 to 6
- query_states: bfloat16 [65536, 5120], P('dp', 'tensor'), may hold values from -96 to 96
- key_states: bfloat16 [65536, 1024], P('dp', 'tensor'), may hold values from -12 to 12
- value_states: bfloat16 [65536, 1024], P('dp', 'tensor'), may hold values from -6 to 6
- output_grad: bfloat16 [65536, 5120], P('dp', 'tensor'), may hold values from -24 to 24
- doc_lengths: int32 [64, 8], P('dp'), may hold values from 0 to 1024, as said below
- send_order: int32 [32, 2], P('dp'), may hold values from 0 to 1, each once within a row
Outputs:
- query_grad: bfloat16 [65536, 5120], P('dp', 'tensor')
- kv_weight_grad: float32 [2048, 5120], P('dp', 'tensor')
The draws below stay inside these ranges and needn't reach their ends.
Inputs may be any that keep to these rules, and one draw needn't show every extreme that they name: `doc_lengths`: each row's 8 lengths sum to at most 1024; the rest of the row is padding. The rows of the last index of dp are full, and the last row of all is a single document.
All inputs are finite; a program needn't handle non-finite values.
Results may differ from the reference program's by a relative error of at most 0.02.
Values may be sent and summed in bfloat16 or wider, within the bound.
A program may use at most 192 MiB of HBM per device.

```python
import jax
import jax.numpy as jnp
from jax import lax

D = 5120
QH = 40
KVH = 8
HD = 128
ROW_LEN = 1024
DOCS = 8
ROWS_DEV = 2
ROWS = 64
TOKENS = 65536
N_DP = 32


def paired_states(key):
    base = jax.random.fold_in(key, 11)
    key_query, key_key = jax.random.split(base, 2)
    keys_wide = jnp.clip(jax.random.normal(key_key, (TOKENS, KVH * HD), jnp.float32), -4.0, 4.0)
    queries_wide = jnp.clip(jax.random.normal(key_query, (TOKENS, QH * HD), jnp.float32), -4.0, 4.0)
    return (queries_wide, keys_wide)


def draw_query_states(key, part):
    return paired_states(key)[0].astype(jnp.bfloat16)


def draw_key_states(key, part):
    return paired_states(key)[1].astype(jnp.bfloat16)


def draw_doc_lengths(key, part):
    rank_count = ROWS // ROWS_DEV
    rank_span = max(rank_count - 1, 1)
    base = jax.random.fold_in(key, 23)
    key_slack, key_cut = jax.random.split(base)
    row_rank = jnp.arange(ROWS, dtype=jnp.int32) // ROWS_DEV
    distance = rank_count - 1 - row_rank
    slack_tokens = jax.random.randint(key_slack, (ROWS,), 0, distance * ROW_LEN // (8 * rank_span) + 1)
    filled = ROW_LEN - distance * 2 * ROW_LEN // (3 * rank_span) - slack_tokens
    cut_points = jnp.sort(jax.random.randint(key_cut, (ROWS, DOCS - 1), 0, filled[:, None] + 1), axis=1)
    last_row = jnp.arange(ROWS) == ROWS - 1
    cut_points = jnp.where(last_row[:, None], ROW_LEN, cut_points)
    boundaries = jnp.concatenate([jnp.zeros((ROWS, 1), jnp.int32), cut_points.astype(jnp.int32), filled[:, None].astype(jnp.int32)], axis=1)
    return jnp.diff(boundaries, axis=1).astype(jnp.int32)


def raised(drawn, key, source, target, parts, factor):
    owner, partner = [(jnp.arange(drawn.shape[axis_at]) // (drawn.shape[axis_at] // parts)).reshape([-1 if axis == axis_at else 1 for axis in range(drawn.ndim)]) for axis_at in (source, target)]
    chosen = jax.random.permutation(key, parts)[partner]
    strong = (owner == chosen) | (owner == (partner + parts // 2) % parts)
    return jnp.where(strong, factor * drawn, drawn)


def shard_levels(rng, dims, pieces, low, top_value):
    def one(axis_at, parts):
        steps = jax.random.uniform(jax.random.fold_in(jax.random.fold_in(rng, 6), axis_at), (parts,), jnp.float32, low / len(pieces), top_value / len(pieces))
        return jnp.repeat(jnp.exp(steps), dims[axis_at] // parts).reshape((-1,) + (1,) * (len(dims) - axis_at - 1))

    factor_of = one(*pieces[0])
    for cut in pieces[1:]:
        factor_of = factor_of * one(*cut)
    return factor_of


def normal_values(own_key, extent, width, reach, cuts=(), kind=jnp.bfloat16):
    values = jax.random.normal(own_key, extent, jnp.float32) * width
    if len(cuts) > 0:
        values = shard_levels(own_key, extent, cuts, -0.22, 0.18) * values
    return jnp.clip(values, min=-reach, max=reach).astype(kind)


def noise_with(stream_key, shape, scale, reach, shards, heavy, kind=jnp.bfloat16):
    values = scale * jax.random.normal(stream_key, shape, jnp.float32)
    if shards:
        values = values * shard_levels(stream_key, shape, shards, -0.22, 0.18)
    return jnp.clip(raised(values, jax.random.fold_in(stream_key, 3), *heavy), -reach, reach).astype(kind)


def setup_inputs(seed: int = 0) -> dict:
    key_list = jax.random.split(jax.random.key(seed), 8)
    layer_input = normal_values(key_list[0], (TOKENS, D), 1.0, 6.0, ((0, 32), (1, 8)))
    query_states = draw_query_states(jax.random.fold_in(key_list[7], 71), 0)
    key_states = draw_key_states(jax.random.fold_in(key_list[7], 71), 0)
    value_states = normal_values(key_list[3], (TOKENS, KVH * HD), 1.0, 6.0, ((0, 32), (1, 8)))
    output_grad = noise_with(key_list[4], (TOKENS, QH * HD), 4.0, 24.0, ((0, 32), (1, 8)), (0, 1, 32, 2.75))
    doc_lengths = draw_doc_lengths(jax.random.fold_in(key_list[7], 71), 0)
    send_order = jax.vmap(lambda own: jax.random.permutation(own, ROWS_DEV))(jax.random.split(key_list[6], N_DP)).reshape((N_DP, ROWS_DEV)).astype(jnp.int32)
    return {"layer_input": layer_input, "query_states": query_states, "key_states": key_states, "value_states": value_states, "output_grad": output_grad, "doc_lengths": doc_lengths, "send_order": send_order}


loss_scale = 256.0
masked_score = -1e30


def segment_ids(doc_lengths):
    boundaries = jnp.cumsum(doc_lengths, axis=1).astype(jnp.int32)
    position = jnp.arange(ROW_LEN, dtype=jnp.int32)
    return jnp.sum((position[None, :, None] >= boundaries[:, None, :]).astype(jnp.int32), axis=2).astype(jnp.int32)


def row_backward(operands):
    query_row, key_row, value_row, grad_row, segment = operands
    group_size = QH // KVH
    score_scale = HD ** -0.5
    query_wide = query_row.astype(jnp.float32).reshape(ROW_LEN, KVH, group_size, HD)
    key_wide = key_row.astype(jnp.float32).reshape(ROW_LEN, KVH, HD)
    value_wide = value_row.astype(jnp.float32).reshape(ROW_LEN, KVH, HD)
    live_token = (segment < DOCS).astype(grad_row.dtype)
    grad_live = grad_row * live_token[:, None]
    grad_wide = grad_live.astype(jnp.float32).reshape(ROW_LEN, KVH, group_size, HD).transpose(1, 2, 0, 3)
    scores = jnp.einsum("qgjd,kgd->gjqk", query_wide, key_wide) * score_scale
    position = jnp.arange(ROW_LEN, dtype=jnp.int32)
    allowed = (position[None, :] <= position[:, None]) & (segment[None, :] == segment[:, None])
    scores = jnp.where(allowed, scores, masked_score)
    row_max = jnp.max(scores, axis=-1, keepdims=True)
    exponent = jnp.exp(scores - row_max)
    attention = exponent / jnp.sum(exponent, axis=-1, keepdims=True)
    attention_low = lax.optimization_barrier(attention.astype(jnp.bfloat16)).astype(jnp.float32)
    outputs = jnp.einsum("gjqk,kgd->gjqd", attention_low, value_wide)
    row_delta = jnp.sum(grad_wide * outputs, axis=-1, keepdims=True)
    grad_attention = jnp.einsum("gjqd,kgd->gjqk", grad_wide, value_wide)
    grad_scores = lax.optimization_barrier((attention * (grad_attention - row_delta)).astype(jnp.bfloat16)).astype(jnp.float32)
    grad_query = (jnp.einsum("gjqk,kgd->qgjd", grad_scores, key_wide) * score_scale).astype(jnp.bfloat16)
    grad_key = (jnp.einsum("gjqk,qgjd->kgd", grad_scores, query_wide) * score_scale).astype(jnp.bfloat16)
    grad_value = jnp.einsum("gjqk,gjqd->kgd", attention_low, grad_wide).astype(jnp.bfloat16)
    stacked = jnp.stack([grad_key, grad_value], axis=2).reshape(ROW_LEN, 2 * KVH * HD)
    return grad_query.reshape(ROW_LEN, QH * HD), stacked


def reference(layer_input, query_states, key_states, value_states, output_grad, doc_lengths, send_order):
    segment = segment_ids(doc_lengths)
    token_total = jnp.sum(doc_lengths).astype(jnp.float32)

    def by_rows(array_in):
        return array_in.reshape(ROWS, ROW_LEN, array_in.shape[1])

    grad_query, kv_grads = lax.map(row_backward, (by_rows(query_states), by_rows(key_states), by_rows(value_states), by_rows(output_grad), segment))
    kv_flat = kv_grads.reshape(TOKENS, 2 * KVH * HD)
    weight_grad = jnp.dot(kv_flat.T, layer_input, preferred_element_type=jnp.float32) * (loss_scale / token_total)
    rank_count = ROWS // ROWS_DEV
    half_count = rank_count // 2
    moved_count = ROWS_DEV // 2
    rank_ids = jnp.arange(rank_count, dtype=jnp.int32)
    partner = ((rank_ids + half_count) % rank_count).astype(jnp.int32)
    kept_rows = send_order[:, moved_count:] + rank_ids[:, None] * ROWS_DEV
    arrived = send_order[partner, :moved_count] + partner[:, None] * ROWS_DEV
    row_order = jnp.concatenate([kept_rows, arrived], axis=1).reshape(-1).astype(jnp.int32)
    query_grad = jnp.take(grad_query, row_order, axis=0).reshape(TOKENS, QH * HD)
    return query_grad, weight_grad
```

```python
import functools
import math

import jax
import jax.numpy as jnp
from jax import lax
from jax.experimental import pallas as pl
from jax.experimental.pallas import tpu as pltpu
from jax.sharding import PartitionSpec as P

QH = 40
KVH = 8
HD = 128
ROW_LEN = 1024
DOCS = 8
GROUP = QH // KVH
BQ = 256

loss_scale = 256.0
masked_score = -1e30
score_scale = HD ** (-0.5)
exp_scale = score_scale * math.log2(math.e)


def attend_block(qb, head, q_ref, g_ref, k_ref, v_ref, kt_ref, start, live, dq_ref, dk_ref, dv_ref):
    q_first = qb * BQ
    length = q_first + BQ
    lanes = pl.ds(pl.multiple_of(head * HD, HD), HD)
    query = q_ref[q_first:length, lanes]
    grad = g_ref[q_first:length, lanes]
    scores = lax.dot_general(
        k_ref[:length, :], query, (((1,), (1,)), ((), ())), preferred_element_type=jnp.float32
    )
    key_index = lax.broadcasted_iota(jnp.int32, (length, BQ), 0)
    query_index = lax.broadcasted_iota(jnp.int32, (1, BQ), 1) + q_first
    allowed = (key_index >= start) & (key_index <= query_index)
    scores = jnp.where(allowed, scores, masked_score)
    top = jnp.max(scores, axis=0, keepdims=True)
    exponent = jnp.exp2((scores - top) * exp_scale)
    total = jnp.sum(exponent, axis=0, keepdims=True)
    grad_probs = lax.dot_general(
        v_ref[:length, :], grad, (((1,), (1,)), ((), ())), preferred_element_type=jnp.float32
    )
    weighted = jnp.sum(exponent * grad_probs, axis=0, keepdims=True)
    inverse = live / total
    delta = weighted / total
    probs = exponent * inverse
    probs_low = probs.astype(jnp.bfloat16)
    grad_scores = (probs * (grad_probs - delta)).astype(jnp.bfloat16)
    dv_ref[:length, :] += jnp.dot(probs_low, grad, preferred_element_type=jnp.float32)
    dk_ref[:length, :] += jnp.dot(grad_scores, query, preferred_element_type=jnp.float32)
    dq_t = jnp.dot(kt_ref[:, :length], grad_scores, preferred_element_type=jnp.float32)
    dq_ref[q_first:length, lanes] = (dq_t.T * score_scale).astype(jnp.bfloat16)


def attention_kernel(
    order_ref, q_ref, k_ref, v_ref, g_ref, start_ref, live_ref, dq_ref, kv_ref, kt_ref, dk_ref, dv_ref
):
    kt_ref[...] = k_ref[0].astype(jnp.float32).T.astype(jnp.bfloat16)
    dk_ref[...] = jnp.zeros_like(dk_ref)
    dv_ref[...] = jnp.zeros_like(dv_ref)

    @pl.loop(0, GROUP)
    def _(head):
        for qb in range(ROW_LEN // BQ):
            columns = slice(qb * BQ, qb * BQ + BQ)
            attend_block(
                qb,
                head,
                q_ref.at[0],
                g_ref.at[0],
                k_ref.at[0],
                v_ref.at[0],
                kt_ref,
                start_ref[0, :, columns],
                live_ref[0, :, columns],
                dq_ref.at[0],
                dk_ref,
                dv_ref,
            )

    kv_ref[0, :, :HD] = (dk_ref[...] * score_scale).astype(jnp.bfloat16)
    kv_ref[0, :, HD:] = dv_ref[...].astype(jnp.bfloat16)


def attention(order, query, key, value, grad, start, live):
    rows = query.shape[0]

    def picked(i, order_ref):
        return (order_ref[i], 0, 0)

    def block(width):
        return pl.BlockSpec((1, ROW_LEN, width), picked)

    return pl.pallas_call(
        attention_kernel,
        out_shape=(
            jax.ShapeDtypeStruct((rows, ROW_LEN, GROUP * HD), jnp.bfloat16),
            jax.ShapeDtypeStruct((rows, ROW_LEN, 2 * HD), jnp.bfloat16),
        ),
        grid_spec=pltpu.PrefetchScalarGridSpec(
            num_scalar_prefetch=1,
            grid=(rows,),
            in_specs=[
                block(GROUP * HD),
                block(HD),
                block(HD),
                block(GROUP * HD),
                pl.BlockSpec((1, 1, ROW_LEN), picked),
                pl.BlockSpec((1, 1, ROW_LEN), picked),
            ],
            out_specs=[
                pl.BlockSpec((1, ROW_LEN, GROUP * HD), lambda i, order_ref: (i, 0, 0)),
                pl.BlockSpec((1, ROW_LEN, 2 * HD), picked),
            ],
            scratch_shapes=[
                pltpu.VMEM((HD, ROW_LEN), jnp.bfloat16),
                pltpu.VMEM((ROW_LEN, HD), jnp.float32),
                pltpu.VMEM((ROW_LEN, HD), jnp.float32),
            ],
        ),
        compiler_params=pltpu.CompilerParams(vmem_limit_bytes=48 << 20),
        name="attention_backward",
    )(order, query, key, value, grad, start, live)


def document_starts(doc_lengths):
    ends = jnp.cumsum(doc_lengths, axis=1)
    position = jnp.arange(ROW_LEN, dtype=jnp.int32)
    passed = position[None, :, None] >= ends[:, None, :]
    start = jnp.max(jnp.where(passed, ends[:, None, :], 0), axis=2)
    live = (position[None, :] < ends[:, -1:]).astype(jnp.float32)
    return start[:, None, :], live[:, None, :]


def shards(
    layer_input, query_states, key_states, value_states, output_grad, doc_lengths, send_order
):
    rows = doc_lengths.shape[0]
    ranks = lax.axis_size("dp")
    half = ranks // 2
    start, live = document_starts(doc_lengths)
    token_total = lax.psum(jnp.sum(doc_lengths).astype(jnp.float32), "dp")

    def by_rows(array_in):
        return array_in.reshape(rows, ROW_LEN, array_in.shape[-1])

    dq, kv = attention(
        send_order[0],
        by_rows(query_states),
        by_rows(key_states),
        by_rows(value_states),
        by_rows(output_grad),
        start,
        live,
    )
    arrived = lax.ppermute(dq[:1], "dp", [(r, (r + half) % ranks) for r in range(ranks)])
    query_grad = jnp.concatenate([dq[1:], arrived], axis=0).reshape(-1, dq.shape[-1])
    all_kv = lax.all_gather(kv.reshape(-1, 2 * HD), "tensor", axis=1, tiled=True)
    partial = lax.dot_general(
        all_kv, layer_input, (((0,), (0,)), ((), ())), preferred_element_type=jnp.float32
    ).astype(jnp.bfloat16)
    summed = lax.psum_scatter(partial, "dp", scatter_dimension=0, tiled=True)
    weight_grad = summed.astype(jnp.float32) * (loss_scale / token_total)
    return (query_grad, weight_grad)


def solution(mesh):
    placed = (P("dp", "tensor"),) * 5 + (P("dp", None),) * 2
    return jax.shard_map(
        shards,
        mesh=mesh,
        in_specs=placed,
        out_specs=(P("dp", "tensor"), P("dp", "tensor")),
        check_vma=False,
    )
```

```python
import math

import jax
import jax.numpy as jnp
from jax import lax
from jax.experimental import pallas as pl
from jax.experimental.pallas import tpu as pltpu
from jax.sharding import PartitionSpec as P

QH = 40
KVH = 8
HD = 128
ROW_LEN = 1024
DOCS = 8
GROUP = QH // KVH
BQ = 256
BLOCKS = ROW_LEN // BQ
ROWS = 2
NX, NY, NZ = 4, 4, 8
NT = 8
WIDTH = GROUP * HD
FEATURES = 2 * HD
PART = FEATURES // NX
HALF = PART // 2
LAG_B = 2
LAG_C = 4

loss_scale = 256.0
masked_score = -1e30
score_scale = HD ** (-0.5)
exp_scale = score_scale * math.log2(math.e)
MESH = pl.DeviceIdType.MESH
f32 = jnp.float32
bf16 = jnp.bfloat16


def attend_block(qb, query, grad, k_ref, v_ref, kt_ref, row, ends, dk_ref, dv_ref):
    q_first = qb * BQ
    length = q_first + BQ
    scores = lax.dot_general(
        k_ref[row, :length, :], query, (((1,), (1,)), ((), ())), preferred_element_type=f32
    )
    query_index = lax.broadcasted_iota(jnp.int32, (1, BQ), 1) + q_first
    start = jnp.zeros((1, BQ), jnp.int32)
    for end in ends:
        start = jnp.where(query_index >= end, end, start)
    live = jnp.where(query_index < ends[-1], 1.0, 0.0).astype(f32)
    key_index = lax.broadcasted_iota(jnp.int32, (length, BQ), 0)
    allowed = (key_index >= start) & (key_index <= query_index)
    scores = jnp.where(allowed, scores, masked_score)
    top = jnp.max(scores, axis=0, keepdims=True)
    exponent = jnp.exp2((scores - top) * exp_scale)
    total = jnp.sum(exponent, axis=0, keepdims=True)
    grad_probs = lax.dot_general(
        v_ref[row, :length, :], grad, (((1,), (1,)), ((), ())), preferred_element_type=f32
    )
    weighted = jnp.sum(exponent * grad_probs, axis=0, keepdims=True)
    inverse = live / total
    delta = weighted / total
    probs = exponent * inverse
    probs_low = probs.astype(bf16)
    grad_scores = (probs * (grad_probs - delta)).astype(bf16)
    dv_ref[:length, :] += jnp.dot(probs_low, grad, preferred_element_type=f32)
    dk_ref[:length, :] += jnp.dot(grad_scores, query, preferred_element_type=f32)
    dq_t = jnp.dot(kt_ref[:, :length], grad_scores, preferred_element_type=f32)
    return (dq_t.T * score_scale).astype(bf16)


def whole_kernel(
    order_ref, lengths_ref, x_hbm, q_hbm, k_hbm, v_hbm, g_hbm,
    dq_hbm, w_ref,
    x_ref, q_ref, k_ref, v_ref, g_ref, kt_ref, dk_ref, dv_ref, dq_ref, kv_ref, wt_ref,
    s1_ref, r1_ref, s2_ref, r2_ref, zs_ref, zr_ref, count_ref, cx_ref, plane_ref, cz_ref,
    in_sem, qg_sem, out_sem, dq_send, dq_recv, g_send, g_recv,
    s1_send, s1_recv, s2_send, s2_recv, z_send, z_recv, cx_send, cx_recv, cz_send, cz_recv,
):
    rank = lax.axis_index("dp")
    lane = lax.axis_index("tensor")
    z, x = rank // NX, rank % NX
    y, c = lane // 2, lane % 2

    def at(dz=0, dx=0, dy=0, dc=0):
        return (
            (z + dz) % NZ * NX + (x + dx) % NX,
            (y + dy) % NY * 2 + (c + dc) % 2,
        )

    def tensor_of(dy, dc):
        return (y + dy) % NY * 2 + (c + dc) % 2

    def remote(src, dst, send, recv, device):
        return pltpu.make_async_remote_copy(
            src_ref=src, dst_ref=dst, send_sem=send, recv_sem=recv, device_id=device,
            device_id_type=MESH,
        )

    def head_lanes(head):
        return pl.ds(pl.multiple_of(head * HD, HD), HD)

    def qg_copies(head):
        lanes = head_lanes(head)
        return [
            pltpu.make_async_copy(q_hbm.at[:, :, lanes], q_ref.at[:, :, lanes], qg_sem.at[0, head]),
            pltpu.make_async_copy(g_hbm.at[:, :, lanes], g_ref.at[:, :, lanes], qg_sem.at[1, head]),
        ]

    k_copy = pltpu.make_async_copy(k_hbm, k_ref, in_sem.at[0])
    v_copy = pltpu.make_async_copy(v_hbm, v_ref, in_sem.at[1])
    x_copy = pltpu.make_async_copy(x_hbm, x_ref, in_sem.at[2])
    k_copy.start()
    for copy in qg_copies(0):
        copy.start()
    v_copy.start()
    for head in range(1, GROUP):
        for copy in qg_copies(head):
            copy.start()
    x_copy.start()

    barrier = pltpu.get_barrier_semaphore()
    peers = [at(dz=j) for j in range(1, NZ)] + [at(dx=j) for j in range(1, NX)]
    peers += [at(dc=1), at(dy=1), at(dy=-1)]
    for peer in peers:
        pl.semaphore_signal(barrier, inc=1, device_id=peer, device_id_type=MESH)
    pl.semaphore_wait(barrier, len(peers))

    tokens = jnp.int32(0)
    for row in range(ROWS):
        for doc in range(DOCS):
            tokens = tokens + lengths_ref[row, doc]
    count_ref[...] = jnp.full((8, 128), tokens, jnp.int32).astype(f32)

    def count_x(j):
        return remote(count_ref, cx_ref.at[j - 1], cx_send.at[j - 1], cx_recv.at[j - 1], at(dx=j))

    def count_z(j):
        return remote(plane_ref, cz_ref.at[j - 1], cz_send.at[j - 1], cz_recv.at[j - 1], at(dz=j))

    for j in range(1, NX):
        count_x(j).start()

    def dq_copy(qb, head):
        lanes = head_lanes(head)
        piece = head * BLOCKS + qb
        return remote(
            dq_ref.at[0, pl.ds(qb * BQ, BQ), lanes],
            dq_hbm.at[1, pl.ds(qb * BQ, BQ), lanes],
            dq_send.at[piece], dq_recv.at[piece], at(dz=NZ // 2),
        )

    def kept_copy():
        return pltpu.make_async_copy(dq_ref.at[1], dq_hbm.at[0], out_sem.at[0])

    def kv_copy(group, index, block, half, device):
        slot, kb = group // BLOCKS, BLOCKS - 1 - group % BLOCKS
        columns = pl.ds(pl.multiple_of(kb * BQ, BQ), BQ)
        features = pl.ds(0, FEATURES) if half is None else pl.ds(half * HD, HD)
        ref = kv_ref.at[slot, block, features, columns]
        return remote(ref, ref, g_send.at[group, index], g_recv.at[group, index], device)

    up, down, other = at(dy=1), at(dy=-1), at(dc=1)

    def own_copies(group):
        mine = tensor_of(0, 0)
        return [
            kv_copy(group, 1, mine, None, up),
            kv_copy(group, 2, mine, None, down),
            kv_copy(group, 0, mine, None, other),
        ]

    def from_below(group):
        return kv_copy(group, 1, tensor_of(-1, 0), None, up)

    def from_above(group):
        return kv_copy(group, 2, tensor_of(1, 0), None, down)

    def forward_copies(group):
        return [
            kv_copy(group, 3, tensor_of(-1, 0), 0, up),
            kv_copy(group, 4, tensor_of(1, 0), 1, down),
            kv_copy(group, 5, tensor_of(-1, 0), None, other),
            kv_copy(group, 6, tensor_of(1, 0), None, other),
        ]

    def far_arrivals(group):
        return [
            kv_copy(group, 3, tensor_of(2, 0), 0, up),
            kv_copy(group, 4, tensor_of(2, 0), 1, down),
        ]

    def far_copies(group):
        return [
            kv_copy(group, 7, tensor_of(2, 0), 0, other),
            kv_copy(group, 8, tensor_of(2, 0), 1, other),
        ]

    def stage_forward(group):
        from_below(group).wait_recv()
        from_above(group).wait_recv()
        for copy in forward_copies(group):
            copy.start()

    def stage_far(group):
        for copy in far_arrivals(group):
            copy.wait_recv()
        for copy in far_copies(group):
            copy.start()

    k_copy.wait()
    v_copy.wait()

    @pl.loop(0, ROWS)
    def _(slot):
        row = order_ref[0, slot]
        kt_ref[...] = k_ref[row].astype(f32).T.astype(bf16)
        dk_ref[...] = jnp.zeros_like(dk_ref)
        dv_ref[...] = jnp.zeros_like(dv_ref)
        ends = []
        running = jnp.int32(0)
        for doc in range(DOCS):
            running = running + lengths_ref[row, doc]
            ends.append(running)
        for qb in reversed(range(BLOCKS)):
            group = slot * BLOCKS + (BLOCKS - 1 - qb)
            tokens_here = slice(qb * BQ, qb * BQ + BQ)

            @pl.loop(0, GROUP)
            def _(head, qb=qb, tokens_here=tokens_here):
                lanes = head_lanes(head)
                if qb == BLOCKS - 1:

                    @pl.when(slot == 0)
                    def _():
                        for copy in qg_copies(head):
                            copy.wait()

                query = jnp.where(
                    row == 0, q_ref[0, tokens_here, lanes], q_ref[1, tokens_here, lanes]
                )
                grad = jnp.where(
                    row == 0, g_ref[0, tokens_here, lanes], g_ref[1, tokens_here, lanes]
                )
                dq_ref[slot, tokens_here, lanes] = attend_block(
                    qb, query, grad,
                    k_ref, v_ref, kt_ref, row, ends, dk_ref, dv_ref,
                )

                @pl.when(slot == 0)
                def _():
                    dq_copy(qb, head).start()

            pair = jnp.concatenate(
                [dk_ref[tokens_here, :] * score_scale, dv_ref[tokens_here, :]], axis=1
            )
            kv_ref[slot, tensor_of(0, 0), :, tokens_here] = pair.T.astype(bf16)
            for copy in own_copies(group):
                copy.start()

            @pl.when(group >= 1)
            def _(group=group):
                stage_forward(group - 1)

            @pl.when(group >= 2)
            def _(group=group):
                stage_far(group - 2)

    kept_copy().start()
    for j in range(1, NX):
        count_x(j).wait()
    plane_ref[...] = count_ref[...] + cx_ref[0] + cx_ref[1] + cx_ref[2]
    for j in range(1, NZ):
        count_z(j).start()
    x_copy.wait()
    groups = ROWS * BLOCKS

    def block_of(i):
        shift = jnp.where(i < 2, 0, jnp.where(i < 4, 1, jnp.where(i < 6, 3, 2)))
        return (y + shift) % NY * 2 + (c + i) % 2

    def s1_copy(i, way):
        return remote(
            s1_ref.at[i, way], r1_ref.at[i, way], s1_send.at[i, way], s1_recv.at[i, way],
            at(dx=1 if way == 0 else -1),
        )

    def s2_copy(i, way):
        return remote(
            s2_ref.at[i, way], r2_ref.at[i, way], s2_send.at[i, way], s2_recv.at[i, way],
            at(dx=1 if way == 0 else -1),
        )

    def z_copy(i):
        block = block_of(i)
        return remote(
            zs_ref.at[i], zr_ref.at[z], z_send.at[i], z_recv.at[z], (block * NX + x, lane)
        )

    def part(i, dx, first=0, size=PART):
        begin = pl.multiple_of((x + dx) % NX * PART + first, HALF)
        return wt_ref[i, pl.ds(begin, size), :]

    first_row, second_row = order_ref[0, 0], order_ref[0, 1]

    @pl.loop(0, NT + LAG_C)
    def _(step):
        @pl.when(step == 1)
        def _():
            @pl.loop(0, groups)
            def _(group):
                kv_copy(group, 0, tensor_of(0, 1), None, other).wait_recv()

        @pl.when(step == 2)
        def _():
            stage_forward(groups - 1)
            stage_far(groups - 2)

        @pl.when(step == 3)
        def _():
            @pl.loop(0, groups)
            def _(group):
                kv_copy(group, 6, tensor_of(1, 1), None, other).wait_recv()

        @pl.when(step == 4)
        def _():
            stage_far(groups - 1)

        @pl.when(step == 5)
        def _():
            @pl.loop(0, groups)
            def _(group):
                kv_copy(group, 5, tensor_of(-1, 1), None, other).wait_recv()

        @pl.when(step == 7)
        def _():
            @pl.loop(0, groups)
            def _(group):
                kv_copy(group, 7, tensor_of(2, 1), 0, other).wait_recv()
                kv_copy(group, 8, tensor_of(2, 1), 1, other).wait_recv()

        @pl.when(step < NT)
        def _():
            block = block_of(step)
            wt_ref[step] = jnp.dot(
                kv_ref[0, block], x_ref[first_row], preferred_element_type=f32
            ) + jnp.dot(kv_ref[1, block], x_ref[second_row], preferred_element_type=f32)
            s1_ref[step, 0] = part(step, 2, 0, HALF).astype(bf16)
            s1_ref[step, 1] = part(step, 2, HALF, HALF).astype(bf16)
            s1_copy(step, 0).start()
            s1_copy(step, 1).start()

        @pl.when((step >= LAG_B) & (step < NT + LAG_B))
        def _():
            i = step - LAG_B
            s1_copy(i, 0).wait_recv()
            s1_copy(i, 1).wait_recv()
            s2_ref[i, 0, :HALF] = (part(i, 1, 0, HALF) + r1_ref[i, 0].astype(f32)).astype(bf16)
            s2_ref[i, 0, HALF:] = part(i, 1, HALF, HALF).astype(bf16)
            s2_ref[i, 1, :HALF] = part(i, -1, 0, HALF).astype(bf16)
            s2_ref[i, 1, HALF:] = (part(i, -1, HALF, HALF) + r1_ref[i, 1].astype(f32)).astype(bf16)
            s2_copy(i, 0).start()
            s2_copy(i, 1).start()

        @pl.when(step >= LAG_C)
        def _():
            i = step - LAG_C
            s2_copy(i, 0).wait_recv()
            s2_copy(i, 1).wait_recv()
            reduced = part(i, 0) + r2_ref[i, 0].astype(f32) + r2_ref[i, 1].astype(f32)

            @pl.when(block_of(i) == z)
            def _():
                w_ref[...] = reduced

            @pl.when(block_of(i) != z)
            def _():
                zs_ref[i] = reduced.astype(bf16)
                z_copy(i).start()

    total = plane_ref[...]
    for j in range(1, NZ):
        count_z(j).wait()
    for j in range(1, NZ):
        total = total + cz_ref[j - 1]
    scale = loss_scale / total[0:1, 0:1]

    @pl.loop(1, NZ)
    def _(j):
        source = (z + j) % NZ
        remote(
            zs_ref.at[0], zr_ref.at[source], z_send.at[0], z_recv.at[source], at(dz=j)
        ).wait_recv()
        w_ref[...] += zr_ref[source].astype(f32)

    w_ref[...] = w_ref[...] * scale

    @pl.loop(0, NT)
    def _(i):
        for way in range(2):
            s1_copy(i, way).wait_send()
            s2_copy(i, way).wait_send()

        @pl.when(block_of(i) != z)
        def _():
            z_copy(i).wait_send()

    @pl.loop(0, groups)
    def _(group):
        for copy in own_copies(group) + forward_copies(group) + far_copies(group):
            copy.wait_send()

    kept_copy().wait()

    @pl.loop(0, GROUP)
    def _(head):
        for qb in range(BLOCKS):
            dq_copy(qb, head).wait()


def shards(
    layer_input, query_states, key_states, value_states, output_grad, doc_lengths, send_order
):
    def by_rows(array_in):
        return array_in.reshape(ROWS, ROW_LEN, array_in.shape[-1])

    anywhere = pl.BlockSpec(memory_space=pl.ANY)
    scalars = pl.BlockSpec(memory_space=pltpu.SMEM)
    dma = pltpu.SemaphoreType.DMA
    query_grad, weight_grad = pl.pallas_call(
        whole_kernel,
        out_shape=(
            jax.ShapeDtypeStruct((ROWS, ROW_LEN, WIDTH), bf16),
            jax.ShapeDtypeStruct((PART, WIDTH), f32),
        ),
        in_specs=[scalars, scalars] + [anywhere] * 5,
        out_specs=[anywhere, pl.BlockSpec(memory_space=pltpu.VMEM)],
        scratch_shapes=[
            pltpu.VMEM((ROWS, ROW_LEN, WIDTH), bf16),
            pltpu.VMEM((ROWS, ROW_LEN, WIDTH), bf16),
            pltpu.VMEM((ROWS, ROW_LEN, HD), bf16),
            pltpu.VMEM((ROWS, ROW_LEN, HD), bf16),
            pltpu.VMEM((ROWS, ROW_LEN, WIDTH), bf16),
            pltpu.VMEM((HD, ROW_LEN), bf16),
            pltpu.VMEM((ROW_LEN, HD), f32),
            pltpu.VMEM((ROW_LEN, HD), f32),
            pltpu.VMEM((ROWS, ROW_LEN, WIDTH), bf16),
            pltpu.VMEM((ROWS, NT, FEATURES, ROW_LEN), bf16),
            pltpu.VMEM((NT, FEATURES, WIDTH), f32),
            pltpu.VMEM((NT, 2, HALF, WIDTH), bf16),
            pltpu.VMEM((NT, 2, HALF, WIDTH), bf16),
            pltpu.VMEM((NT, 2, PART, WIDTH), bf16),
            pltpu.VMEM((NT, 2, PART, WIDTH), bf16),
            pltpu.VMEM((NT, PART, WIDTH), bf16),
            pltpu.VMEM((NZ, PART, WIDTH), bf16),
            pltpu.VMEM((8, 128), f32),
            pltpu.VMEM((NX - 1, 8, 128), f32),
            pltpu.VMEM((8, 128), f32),
            pltpu.VMEM((NZ - 1, 8, 128), f32),
            dma((3,)),
            dma((2, GROUP)),
            dma((1,)),
            dma((GROUP * BLOCKS,)),
            dma((GROUP * BLOCKS,)),
            dma((ROWS * BLOCKS, 9)),
            dma((ROWS * BLOCKS, 9)),
            dma((NT, 2)),
            dma((NT, 2)),
            dma((NT, 2)),
            dma((NT, 2)),
            dma((NT,)),
            dma((NZ,)),
            dma((NX - 1,)),
            dma((NX - 1,)),
            dma((NZ - 1,)),
            dma((NZ - 1,)),
        ],
        compiler_params=pltpu.CompilerParams(
            collective_id=0, has_side_effects=True, vmem_limit_bytes=60 << 20
        ),
        name="attention_backward_and_weight_grad",
    )(
        send_order,
        doc_lengths,
        by_rows(layer_input),
        by_rows(query_states),
        by_rows(key_states),
        by_rows(value_states),
        by_rows(output_grad),
    )
    return (query_grad.reshape(-1, WIDTH), weight_grad)


def solution(mesh):
    placed = (P("dp", "tensor"),) * 5 + (P("dp", None),) * 2
    return jax.shard_map(
        shards,
        mesh=mesh,
        in_specs=placed,
        out_specs=(P("dp", "tensor"), P("dp", "tensor")),
        check_vma=False,
    )
```

```python
import math

import jax
import jax.numpy as jnp
from jax import lax
from jax.experimental import pallas as pl
from jax.experimental.pallas import tpu as pltpu
from jax.sharding import PartitionSpec as P

QH = 40
KVH = 8
HD = 128
ROW_LEN = 1024
DOCS = 8
GROUP = QH // KVH
BQ = 256
BLOCKS = ROW_LEN // BQ
ROWS = 2
NX, NY, NZ = 4, 4, 8
NT = 8
WIDTH = GROUP * HD
FEATURES = 2 * HD
PART = FEATURES // NX
HALF = PART // 2
LAG_B = 1
LAG_C = 3

loss_scale = 256.0
masked_score = -1e30
score_scale = HD ** (-0.5)
exp_scale = score_scale * math.log2(math.e)
MESH = pl.DeviceIdType.MESH
DURING = {5: ((0, 0), (0, 1), (0, 2)), 6: ((1, 0),), 7: ((0, 3), (1, 1), (1, 2))}
f32 = jnp.float32
bf16 = jnp.bfloat16


def dot_nt(left, right):
    return lax.dot_general(left, right, (((1,), (1,)), ((), ())), preferred_element_type=f32)


def first_pass(offset, diagonal, scores, grad_probs, start, query_index):
    key_index = lax.broadcasted_iota(jnp.int32, (BQ, BQ), 0)
    allowed = key_index >= start - offset
    if diagonal:
        allowed = allowed & (key_index <= query_index - offset)
    scores = jnp.where(allowed, scores, masked_score)
    top = jnp.max(scores, axis=0, keepdims=True)
    exponent = jnp.exp2((scores - top) * exp_scale)
    return (
        exponent,
        grad_probs,
        top,
        jnp.sum(exponent, axis=0, keepdims=True),
        jnp.sum(exponent * grad_probs, axis=0, keepdims=True),
    )


def tile_scales(parts, live):
    top = parts[0][2]
    for part in parts[1:]:
        top = jnp.maximum(top, part[2])
    shift = [jnp.exp2((part[2] - top) * exp_scale) for part in parts]
    total = sum(by * part[3] for by, part in zip(shift, parts))
    weighted = sum(by * part[4] for by, part in zip(shift, parts))
    inverse = live / total
    return [inverse * by for by in shift], weighted / total


def attend_group(qb, load, k_ref, v_ref, kt_ref, row, ends, dk_ref, dv_ref, store):
    q_first = qb * BQ
    query_index = lax.broadcasted_iota(jnp.int32, (1, BQ), 1) + q_first
    start = jnp.zeros((1, BQ), jnp.int32)
    for end in ends:
        start = jnp.where(query_index >= end, end, start)
    live = jnp.where(query_index < ends[-1], 1.0, 0.0).astype(f32)
    before = None
    for head in range(GROUP + 1):
        now = None
        if head < GROUP:
            query, grad = load(head)
            now = (query, grad, [])
        if before is not None:
            scales, delta = tile_scales(before[2], live)
            dq_t = jnp.zeros((HD, BQ), f32)
        for tile in range(qb + 1):
            keys = slice(tile * BQ, tile * BQ + BQ)
            if now is not None:
                scores = dot_nt(k_ref[row, keys, :], query)
                grad_probs = dot_nt(v_ref[row, keys, :], grad)
            if before is not None:
                probs = before[2][tile][0] * scales[tile]
                grad_scores = (probs * (before[2][tile][1] - delta)).astype(bf16)
                dv_ref[keys, :] += jnp.dot(
                    probs.astype(bf16), before[1], preferred_element_type=f32
                )
                dk_ref[keys, :] += jnp.dot(grad_scores, before[0], preferred_element_type=f32)
                dq_t = dq_t + jnp.dot(kt_ref[:, keys], grad_scores, preferred_element_type=f32)
            if now is not None:
                now[2].append(
                    first_pass(tile * BQ, tile == qb, scores, grad_probs, start, query_index)
                )
        if before is not None:
            store(head - 1, (dq_t.T * score_scale).astype(bf16))
        before = now


def whole_kernel(
    order_ref, lengths_ref, x_hbm, q_hbm, k_hbm, v_hbm, g_hbm,
    dq_hbm, w_ref,
    x_ref, q_ref, k_ref, v_ref, g_ref, kt_ref, dk_ref, dv_ref, dq_ref, kv_ref, wt_ref,
    s1_ref, r1_ref, s2_ref, r2_ref, zs_ref, zr_ref, count_ref, cx_ref, plane_ref, cz_ref,
    in_sem, qg_sem, out_sem, dq_send, dq_recv, g_send, g_recv,
    s1_send, s1_recv, s2_send, s2_recv, z_send, z_recv, cx_send, cx_recv, cz_send, cz_recv,
):
    rank = lax.axis_index("dp")
    lane = lax.axis_index("tensor")
    z, x = rank // NX, rank % NX
    y, c = lane // 2, lane % 2

    def at(dz=0, dx=0, dy=0, dc=0):
        return (
            (z + dz) % NZ * NX + (x + dx) % NX,
            (y + dy) % NY * 2 + (c + dc) % 2,
        )

    def tensor_of(dy, dc):
        return (y + dy) % NY * 2 + (c + dc) % 2

    def remote(src, dst, send, recv, device):
        return pltpu.make_async_remote_copy(
            src_ref=src, dst_ref=dst, send_sem=send, recv_sem=recv, device_id=device,
            device_id_type=MESH,
        )

    def head_lanes(head):
        if isinstance(head, int):
            return pl.ds(head * HD, HD)
        return pl.ds(pl.multiple_of(head * HD, HD), HD)

    def qg_copies(head):
        lanes = head_lanes(head)
        return [
            pltpu.make_async_copy(q_hbm.at[:, :, lanes], q_ref.at[:, :, lanes], qg_sem.at[0, head]),
            pltpu.make_async_copy(g_hbm.at[:, :, lanes], g_ref.at[:, :, lanes], qg_sem.at[1, head]),
        ]

    k_copy = pltpu.make_async_copy(k_hbm, k_ref, in_sem.at[0])
    v_copy = pltpu.make_async_copy(v_hbm, v_ref, in_sem.at[1])
    x_copy = pltpu.make_async_copy(x_hbm, x_ref, in_sem.at[2])
    k_copy.start()
    for copy in qg_copies(0):
        copy.start()
    v_copy.start()
    for head in range(1, GROUP):
        for copy in qg_copies(head):
            copy.start()
    x_copy.start()

    barrier = pltpu.get_barrier_semaphore()
    peers = [at(dz=j) for j in range(1, NZ)] + [at(dx=j) for j in range(1, NX)]
    peers += [at(dc=1), at(dy=1), at(dy=-1)]
    for peer in peers:
        pl.semaphore_signal(barrier, inc=1, device_id=peer, device_id_type=MESH)
    pl.semaphore_wait(barrier, len(peers))

    tokens = jnp.int32(0)
    for row in range(ROWS):
        for doc in range(DOCS):
            tokens = tokens + lengths_ref[row, doc]
    count_ref[...] = jnp.full((8, 128), tokens, jnp.int32).astype(f32)

    def count_x(j):
        return remote(count_ref, cx_ref.at[j - 1], cx_send.at[j - 1], cx_recv.at[j - 1], at(dx=j))

    def count_z(j):
        return remote(plane_ref, cz_ref.at[j - 1], cz_send.at[j - 1], cz_recv.at[j - 1], at(dz=j))

    for j in range(1, NX):
        count_x(j).start()

    def dq_copy(qb, head):
        lanes = head_lanes(head)
        piece = head * BLOCKS + qb
        return remote(
            dq_ref.at[0, pl.ds(qb * BQ, BQ), lanes],
            dq_hbm.at[1, pl.ds(qb * BQ, BQ), lanes],
            dq_send.at[piece], dq_recv.at[piece], at(dz=NZ // 2),
        )

    def kept_copy():
        return pltpu.make_async_copy(dq_ref.at[1], dq_hbm.at[0], out_sem.at[0])

    def kv_copy(group, index, block, half, device):
        slot, kb = group // BLOCKS, BLOCKS - 1 - group % BLOCKS
        features = pl.ds(0, FEATURES) if half is None else pl.ds(half * HD, HD)
        ref = kv_ref.at[slot, kb, block, features]
        return remote(ref, ref, g_send.at[group, index], g_recv.at[group, index], device)

    up, down, other = at(dy=1), at(dy=-1), at(dc=1)

    def own_copies(group):
        mine = tensor_of(0, 0)
        return [
            kv_copy(group, 1, mine, None, up),
            kv_copy(group, 2, mine, None, down),
            kv_copy(group, 0, mine, None, other),
        ]

    def from_below(group):
        return kv_copy(group, 1, tensor_of(-1, 0), None, up)

    def from_above(group):
        return kv_copy(group, 2, tensor_of(1, 0), None, down)

    def forward_copies(group):
        return [
            kv_copy(group, 3, tensor_of(-1, 0), 0, up),
            kv_copy(group, 4, tensor_of(1, 0), 1, down),
            kv_copy(group, 5, tensor_of(-1, 0), None, other),
            kv_copy(group, 6, tensor_of(1, 0), None, other),
        ]

    def far_arrivals(group):
        return [
            kv_copy(group, 3, tensor_of(2, 0), 0, up),
            kv_copy(group, 4, tensor_of(2, 0), 1, down),
        ]

    def far_copies(group):
        return [
            kv_copy(group, 7, tensor_of(2, 0), 0, other),
            kv_copy(group, 8, tensor_of(2, 0), 1, other),
        ]

    def stage_forward(group):
        from_below(group).wait_recv()
        from_above(group).wait_recv()
        for copy in forward_copies(group):
            copy.start()

    def stage_far(group):
        for copy in far_arrivals(group):
            copy.wait_recv()
        for copy in far_copies(group):
            copy.start()

    k_copy.wait()
    v_copy.wait()

    for slot in range(ROWS):
        row = order_ref[0, slot]
        kt_ref[...] = k_ref[row].astype(f32).T.astype(bf16)
        dk_ref[...] = jnp.zeros_like(dk_ref)
        dv_ref[...] = jnp.zeros_like(dv_ref)
        ends = []
        running = jnp.int32(0)
        for doc in range(DOCS):
            running = running + lengths_ref[row, doc]
            ends.append(running)
        for qb in reversed(range(BLOCKS)):
            group = slot * BLOCKS + (BLOCKS - 1 - qb)
            tokens_here = slice(qb * BQ, qb * BQ + BQ)

            def load(head):
                lanes = slice(head * HD, head * HD + HD)
                if slot == 0 and qb == BLOCKS - 1:
                    for copy in qg_copies(head):
                        copy.wait()
                return (
                    jnp.where(row == 0, q_ref[0, tokens_here, lanes], q_ref[1, tokens_here, lanes]),
                    jnp.where(row == 0, g_ref[0, tokens_here, lanes], g_ref[1, tokens_here, lanes]),
                )

            def store(head, piece):
                dq_ref[slot, tokens_here, head * HD : head * HD + HD] = piece
                if slot == 0:
                    dq_copy(qb, head).start()

            attend_group(qb, load, k_ref, v_ref, kt_ref, row, ends, dk_ref, dv_ref, store)
            pair = jnp.concatenate(
                [dk_ref[tokens_here, :] * score_scale, dv_ref[tokens_here, :]], axis=1
            )
            kv_ref[slot, qb, tensor_of(0, 0)] = pair.T.astype(bf16)
            for copy in own_copies(group):
                copy.start()
            for stage, ready in DURING.get(group, ()):
                (stage_forward if stage == 0 else stage_far)(ready)

    kept_copy().start()
    for j in range(1, NX):
        count_x(j).wait()
    plane_ref[...] = count_ref[...] + cx_ref[0] + cx_ref[1] + cx_ref[2]
    for j in range(1, NZ):
        count_z(j).start()
    x_copy.wait()
    groups = ROWS * BLOCKS

    def block_of(i):
        shift = jnp.where(i < 2, 0, jnp.where(i < 4, 1, jnp.where(i < 6, 3, 2)))
        return (y + shift) % NY * 2 + (c + i) % 2

    def s1_copy(i, way):
        return remote(
            s1_ref.at[i, way], r1_ref.at[i, way], s1_send.at[i, way], s1_recv.at[i, way],
            at(dx=1 if way == 0 else -1),
        )

    def s2_copy(i, way):
        return remote(
            s2_ref.at[i, way], r2_ref.at[i, way], s2_send.at[i, way], s2_recv.at[i, way],
            at(dx=1 if way == 0 else -1),
        )

    def z_copy(i):
        block = block_of(i)
        return remote(
            zs_ref.at[i], zr_ref.at[z], z_send.at[i], z_recv.at[z], (block * NX + x, lane)
        )

    def part(i, dx, first=0, size=PART):
        begin = pl.multiple_of((x + dx) % NX * PART + first, HALF)
        return wt_ref[i, pl.ds(begin, size), :]

    first_row, second_row = order_ref[0, 0], order_ref[0, 1]

    def own_part(step):
        i = jnp.where(step < 2, step, step - 2)
        return i, (step >= 0) & (i < NT) & ((step < 2) | (step >= 4))

    def gathered(slot, block):
        return jnp.concatenate([kv_ref[slot, kb, block] for kb in range(BLOCKS)], axis=1)

    def wait_group(index, block, half=None):
        @pl.loop(0, groups)
        def _(group):
            kv_copy(group, index, block, half, other).wait_recv()

    @pl.loop(0, NT + 2 + LAG_C)
    def _(step):
        i_a, go_a = own_part(step)

        @pl.when(go_a)
        def _():
            block = block_of(i_a)
            wt_ref[i_a] = jnp.dot(
                gathered(0, block), x_ref[first_row], preferred_element_type=f32
            ) + jnp.dot(gathered(1, block), x_ref[second_row], preferred_element_type=f32)
            s1_ref[i_a, 0] = part(i_a, 2, 0, HALF).astype(bf16)
            s1_ref[i_a, 1] = part(i_a, 2, HALF, HALF).astype(bf16)
            s1_copy(i_a, 0).start()
            s1_copy(i_a, 1).start()

        i_b, go_b = own_part(step - LAG_B)

        @pl.when(go_b)
        def _():
            i = i_b
            s1_copy(i, 0).wait_recv()
            s1_copy(i, 1).wait_recv()
            s2_ref[i, 0, :HALF] = (part(i, 1, 0, HALF) + r1_ref[i, 0].astype(f32)).astype(bf16)
            s2_ref[i, 0, HALF:] = part(i, 1, HALF, HALF).astype(bf16)
            s2_ref[i, 1, :HALF] = part(i, -1, 0, HALF).astype(bf16)
            s2_ref[i, 1, HALF:] = (part(i, -1, HALF, HALF) + r1_ref[i, 1].astype(f32)).astype(bf16)
            s2_copy(i, 0).start()
            s2_copy(i, 1).start()

        i_c, go_c = own_part(step - LAG_C)

        @pl.when(go_c)
        def _():
            i = i_c
            s2_copy(i, 0).wait_recv()
            s2_copy(i, 1).wait_recv()
            reduced = part(i, 0) + r2_ref[i, 0].astype(f32) + r2_ref[i, 1].astype(f32)

            @pl.when(block_of(i) == z)
            def _():
                w_ref[...] = reduced

            @pl.when(block_of(i) != z)
            def _():
                zs_ref[i] = reduced.astype(bf16)
                z_copy(i).start()

        @pl.when(step == 0)
        def _():
            wait_group(0, tensor_of(0, 1))

        @pl.when(step == 1)
        def _():
            stage_forward(4)
            stage_far(3)

        @pl.when(step == 2)
        def _():
            stage_forward(5)
            stage_far(4)
            stage_forward(6)

        @pl.when(step == 3)
        def _():
            stage_far(5)
            stage_forward(7)

        @pl.when(step == 4)
        def _():
            stage_far(6)
            wait_group(6, tensor_of(1, 1))

        @pl.when(step == 5)
        def _():
            stage_far(7)

        @pl.when(step == 6)
        def _():
            wait_group(5, tensor_of(-1, 1))

        @pl.when(step == 8)
        def _():
            wait_group(7, tensor_of(2, 1), 0)
            wait_group(8, tensor_of(2, 1), 1)

    total = plane_ref[...]
    for j in range(1, NZ):
        count_z(j).wait()
    for j in range(1, NZ):
        total = total + cz_ref[j - 1]
    scale = loss_scale / total[0:1, 0:1]

    @pl.loop(1, NZ)
    def _(j):
        source = (z + j) % NZ
        remote(
            zs_ref.at[0], zr_ref.at[source], z_send.at[0], z_recv.at[source], at(dz=j)
        ).wait_recv()
        w_ref[...] += zr_ref[source].astype(f32)

    w_ref[...] = w_ref[...] * scale

    @pl.loop(0, NT)
    def _(i):
        for way in range(2):
            s1_copy(i, way).wait_send()
            s2_copy(i, way).wait_send()

        @pl.when(block_of(i) != z)
        def _():
            z_copy(i).wait_send()

    @pl.loop(0, groups)
    def _(group):
        for copy in own_copies(group) + forward_copies(group) + far_copies(group):
            copy.wait_send()

    kept_copy().wait()

    @pl.loop(0, GROUP)
    def _(head):
        for qb in range(BLOCKS):
            dq_copy(qb, head).wait()


def shards(
    layer_input, query_states, key_states, value_states, output_grad, doc_lengths, send_order
):
    def by_rows(array_in):
        return array_in.reshape(ROWS, ROW_LEN, array_in.shape[-1])

    anywhere = pl.BlockSpec(memory_space=pl.ANY)
    scalars = pl.BlockSpec(memory_space=pltpu.SMEM)
    dma = pltpu.SemaphoreType.DMA
    query_grad, weight_grad = pl.pallas_call(
        whole_kernel,
        out_shape=(
            jax.ShapeDtypeStruct((ROWS, ROW_LEN, WIDTH), bf16),
            jax.ShapeDtypeStruct((PART, WIDTH), f32),
        ),
        in_specs=[scalars, scalars] + [anywhere] * 5,
        out_specs=[anywhere, pl.BlockSpec(memory_space=pltpu.VMEM)],
        scratch_shapes=[
            pltpu.VMEM((ROWS, ROW_LEN, WIDTH), bf16),
            pltpu.VMEM((ROWS, ROW_LEN, WIDTH), bf16),
            pltpu.VMEM((ROWS, ROW_LEN, HD), bf16),
            pltpu.VMEM((ROWS, ROW_LEN, HD), bf16),
            pltpu.VMEM((ROWS, ROW_LEN, WIDTH), bf16),
            pltpu.VMEM((HD, ROW_LEN), bf16),
            pltpu.VMEM((ROW_LEN, HD), f32),
            pltpu.VMEM((ROW_LEN, HD), f32),
            pltpu.VMEM((ROWS, ROW_LEN, WIDTH), bf16),
            pltpu.VMEM((ROWS, BLOCKS, NT, FEATURES, BQ), bf16),
            pltpu.VMEM((NT, FEATURES, WIDTH), f32),
            pltpu.VMEM((NT, 2, HALF, WIDTH), bf16),
            pltpu.VMEM((NT, 2, HALF, WIDTH), bf16),
            pltpu.VMEM((NT, 2, PART, WIDTH), bf16),
            pltpu.VMEM((NT, 2, PART, WIDTH), bf16),
            pltpu.VMEM((NT, PART, WIDTH), bf16),
            pltpu.VMEM((NZ, PART, WIDTH), bf16),
            pltpu.VMEM((8, 128), f32),
            pltpu.VMEM((NX - 1, 8, 128), f32),
            pltpu.VMEM((8, 128), f32),
            pltpu.VMEM((NZ - 1, 8, 128), f32),
            dma((3,)),
            dma((2, GROUP)),
            dma((1,)),
            dma((GROUP * BLOCKS,)),
            dma((GROUP * BLOCKS,)),
            dma((ROWS * BLOCKS, 9)),
            dma((ROWS * BLOCKS, 9)),
            dma((NT, 2)),
            dma((NT, 2)),
            dma((NT, 2)),
            dma((NT, 2)),
            dma((NT,)),
            dma((NZ,)),
            dma((NX - 1,)),
            dma((NX - 1,)),
            dma((NZ - 1,)),
            dma((NZ - 1,)),
        ],
        compiler_params=pltpu.CompilerParams(
            collective_id=0, has_side_effects=True, vmem_limit_bytes=60 << 20
        ),
        name="attention_backward_and_weight_grad",
    )(
        send_order,
        doc_lengths,
        by_rows(layer_input),
        by_rows(query_states),
        by_rows(key_states),
        by_rows(value_states),
        by_rows(output_grad),
    )
    return (query_grad.reshape(-1, WIDTH), weight_grad)


def solution(mesh):
    placed = (P("dp", "tensor"),) * 5 + (P("dp", None),) * 2
    return jax.shard_map(
        shards,
        mesh=mesh,
        in_specs=placed,
        out_specs=(P("dp", "tensor"), P("dp", "tensor")),
        check_vma=False,
    )
```

```python
import math

import jax
import jax.numpy as jnp
from jax import lax
from jax.experimental import pallas as pl
from jax.experimental.pallas import tpu as pltpu
from jax.sharding import PartitionSpec as P

QH = 40
KVH = 8
HD = 128
ROW_LEN = 1024
DOCS = 8
GROUP = QH // KVH
BQ = 256
BLOCKS = ROW_LEN // BQ
ROWS = 2
NX, NY, NZ = 4, 4, 8
NT = 8
WIDTH = GROUP * HD
FEATURES = 2 * HD
PART = FEATURES // NX
HALF = PART // 2
LAG_B = 1
LAG_C = 3

loss_scale = 256.0
masked_score = -1e30
score_scale = HD ** (-0.5)
exp_scale = score_scale * math.log2(math.e)
MESH = pl.DeviceIdType.MESH
DURING = {5: ((0, 0), (0, 1), (0, 2)), 6: ((0, 3),), 7: ((0, 4),)}
f32 = jnp.float32
bf16 = jnp.bfloat16


def dot_nt(left, right):
    return lax.dot_general(left, right, (((1,), (1,)), ((), ())), preferred_element_type=f32)


def first_pass(offset, diagonal, scores, grad_probs, start, query_index):
    key_index = lax.broadcasted_iota(jnp.int32, (BQ, BQ), 0)
    allowed = key_index >= start - offset
    if diagonal:
        allowed = allowed & (key_index <= query_index - offset)
    scores = jnp.where(allowed, scores, masked_score)
    top = jnp.max(scores, axis=0, keepdims=True)
    exponent = jnp.exp2((scores - top) * exp_scale)
    return (
        exponent,
        grad_probs,
        top,
        jnp.sum(exponent, axis=0, keepdims=True),
        jnp.sum(exponent * grad_probs, axis=0, keepdims=True),
    )


def tile_scales(parts, live):
    top = parts[0][2]
    for part in parts[1:]:
        top = jnp.maximum(top, part[2])
    shift = [jnp.exp2((part[2] - top) * exp_scale) for part in parts]
    total = sum(by * part[3] for by, part in zip(shift, parts))
    weighted = sum(by * part[4] for by, part in zip(shift, parts))
    inverse = live / total
    return [inverse * by for by in shift], weighted / total


def attend_group(qb, load, k_ref, v_ref, kt_ref, row, ends, dk_ref, dv_ref, store):
    q_first = qb * BQ
    query_index = lax.broadcasted_iota(jnp.int32, (1, BQ), 1) + q_first
    start = jnp.zeros((1, BQ), jnp.int32)
    for end in ends:
        start = jnp.where(query_index >= end, end, start)
    live = jnp.where(query_index < ends[-1], 1.0, 0.0).astype(f32)
    before = None
    for head in range(GROUP + 1):
        now = None
        if head < GROUP:
            query, grad = load(head)
            now = (query, grad, [])
        if before is not None:
            scales, delta = tile_scales(before[2], live)
            dq_t = jnp.zeros((HD, BQ), f32)
        for tile in range(qb + 1):
            keys = slice(tile * BQ, tile * BQ + BQ)
            if now is not None:
                scores = dot_nt(k_ref[row, keys, :], query)
                grad_probs = dot_nt(v_ref[row, keys, :], grad)
            if before is not None:
                probs = before[2][tile][0] * scales[tile]
                grad_scores = (probs * (before[2][tile][1] - delta)).astype(bf16)
                dv_ref[keys, :] += jnp.dot(
                    probs.astype(bf16), before[1], preferred_element_type=f32
                )
                dk_ref[keys, :] += jnp.dot(grad_scores, before[0], preferred_element_type=f32)
                dq_t = dq_t + jnp.dot(kt_ref[:, keys], grad_scores, preferred_element_type=f32)
            if now is not None:
                now[2].append(
                    first_pass(tile * BQ, tile == qb, scores, grad_probs, start, query_index)
                )
        if before is not None:
            store(head - 1, (dq_t.T * score_scale).astype(bf16))
        before = now


def whole_kernel(
    order_ref, lengths_ref, x_hbm, q_hbm, k_hbm, v_hbm, g_hbm,
    dq_hbm, w_ref,
    x_ref, q_ref, k_ref, v_ref, g_ref, kt_ref, dk_ref, dv_ref, dq_ref, kv_ref, wt_ref,
    s1_ref, r1_ref, s2_ref, r2_ref, zs_ref, zr_ref, count_ref, cx_ref, plane_ref, cz_ref,
    in_sem, qg_sem, out_sem, dq_send, dq_recv, g_send, g_recv,
    s1_send, s1_recv, s2_send, s2_recv, z_send, z_recv, cx_send, cx_recv, cz_send, cz_recv,
):
    rank = lax.axis_index("dp")
    lane = lax.axis_index("tensor")
    z, x = rank // NX, rank % NX
    y, c = lane // 2, lane % 2

    def at(dz=0, dx=0, dy=0, dc=0):
        return (
            (z + dz) % NZ * NX + (x + dx) % NX,
            (y + dy) % NY * 2 + (c + dc) % 2,
        )

    def tensor_of(dy, dc):
        return (y + dy) % NY * 2 + (c + dc) % 2

    def remote(src, dst, send, recv, device):
        return pltpu.make_async_remote_copy(
            src_ref=src, dst_ref=dst, send_sem=send, recv_sem=recv, device_id=device,
            device_id_type=MESH,
        )

    def head_lanes(head):
        if isinstance(head, int):
            return pl.ds(head * HD, HD)
        return pl.ds(pl.multiple_of(head * HD, HD), HD)

    def qg_copies(head):
        lanes = head_lanes(head)
        return [
            pltpu.make_async_copy(q_hbm.at[:, :, lanes], q_ref.at[:, :, lanes], qg_sem.at[0, head]),
            pltpu.make_async_copy(g_hbm.at[:, :, lanes], g_ref.at[:, :, lanes], qg_sem.at[1, head]),
        ]

    k_copy = pltpu.make_async_copy(k_hbm, k_ref, in_sem.at[0])
    v_copy = pltpu.make_async_copy(v_hbm, v_ref, in_sem.at[1])
    x_copy = pltpu.make_async_copy(x_hbm, x_ref, in_sem.at[2])
    k_copy.start()
    for copy in qg_copies(0):
        copy.start()
    v_copy.start()
    for head in range(1, GROUP):
        for copy in qg_copies(head):
            copy.start()
    x_copy.start()

    barrier = pltpu.get_barrier_semaphore()
    peers = [at(dz=j) for j in range(1, NZ)] + [at(dx=j) for j in range(1, NX)]
    peers += [at(dc=1), at(dy=1), at(dy=-1)]
    for peer in peers:
        pl.semaphore_signal(barrier, inc=1, device_id=peer, device_id_type=MESH)
    pl.semaphore_wait(barrier, len(peers))

    tokens = jnp.int32(0)
    for row in range(ROWS):
        for doc in range(DOCS):
            tokens = tokens + lengths_ref[row, doc]
    count_ref[...] = jnp.full((8, 128), tokens, jnp.int32).astype(f32)

    def count_x(j):
        return remote(count_ref, cx_ref.at[j - 1], cx_send.at[j - 1], cx_recv.at[j - 1], at(dx=j))

    def count_z(j):
        return remote(plane_ref, cz_ref.at[j - 1], cz_send.at[j - 1], cz_recv.at[j - 1], at(dz=j))

    for j in range(1, NX):
        count_x(j).start()

    def dq_copy(qb, head):
        lanes = head_lanes(head)
        piece = head * BLOCKS + qb
        return remote(
            dq_ref.at[0, pl.ds(qb * BQ, BQ), lanes],
            dq_hbm.at[1, pl.ds(qb * BQ, BQ), lanes],
            dq_send.at[piece], dq_recv.at[piece], at(dz=NZ // 2),
        )

    def kept_copy():
        return pltpu.make_async_copy(dq_ref.at[1], dq_hbm.at[0], out_sem.at[0])

    def kv_copy(group, index, block, half, device):
        slot, kb = group // BLOCKS, BLOCKS - 1 - group % BLOCKS
        features = pl.ds(0, FEATURES) if half is None else pl.ds(half * HD, HD)
        ref = kv_ref.at[slot, kb, block, features]
        return remote(ref, ref, g_send.at[group, index], g_recv.at[group, index], device)

    up, down, other = at(dy=1), at(dy=-1), at(dc=1)

    def own_copies(group):
        mine = tensor_of(0, 0)
        return [
            kv_copy(group, 1, mine, None, up),
            kv_copy(group, 2, mine, None, down),
            kv_copy(group, 0, mine, None, other),
        ]

    def from_below(group):
        return kv_copy(group, 1, tensor_of(-1, 0), None, up)

    def from_above(group):
        return kv_copy(group, 2, tensor_of(1, 0), None, down)

    def forward_copies(group):
        return [
            kv_copy(group, 3, tensor_of(-1, 0), 0, up),
            kv_copy(group, 4, tensor_of(1, 0), 1, down),
            kv_copy(group, 5, tensor_of(-1, 0), None, other),
            kv_copy(group, 6, tensor_of(1, 0), None, other),
        ]

    def far_arrivals(group):
        return [
            kv_copy(group, 3, tensor_of(2, 0), 0, up),
            kv_copy(group, 4, tensor_of(2, 0), 1, down),
        ]

    def far_copies(group):
        return [
            kv_copy(group, 7, tensor_of(2, 0), 0, other),
            kv_copy(group, 8, tensor_of(2, 0), 1, other),
        ]

    def stage_forward(group):
        from_below(group).wait_recv()
        from_above(group).wait_recv()
        for copy in forward_copies(group):
            copy.start()

    def stage_far(group):
        for copy in far_arrivals(group):
            copy.wait_recv()
        for copy in far_copies(group):
            copy.start()

    k_copy.wait()
    v_copy.wait()

    for slot in range(ROWS):
        row = order_ref[0, slot]
        kt_ref[...] = k_ref[row].astype(f32).T.astype(bf16)
        dk_ref[...] = jnp.zeros_like(dk_ref)
        dv_ref[...] = jnp.zeros_like(dv_ref)
        ends = []
        running = jnp.int32(0)
        for doc in range(DOCS):
            running = running + lengths_ref[row, doc]
            ends.append(running)
        for qb in (0, 3, 2, 1) if slot == 0 else (3, 2, 1, 0):
            tokens_here = slice(qb * BQ, qb * BQ + BQ)

            def load(head):
                lanes = slice(head * HD, head * HD + HD)
                if slot == 0 and qb == 0:
                    for copy in qg_copies(head):
                        copy.wait()
                return (
                    jnp.where(row == 0, q_ref[0, tokens_here, lanes], q_ref[1, tokens_here, lanes]),
                    jnp.where(row == 0, g_ref[0, tokens_here, lanes], g_ref[1, tokens_here, lanes]),
                )

            def store(head, piece):
                dq_ref[slot, tokens_here, head * HD : head * HD + HD] = piece
                if slot == 0:
                    dq_copy(qb, head).start()

            attend_group(qb, load, k_ref, v_ref, kt_ref, row, ends, dk_ref, dv_ref, store)
            final = (qb,)
            if slot == 0:
                final = {0: (), 1: (1, 0)}.get(qb, (qb,))
            group = None
            for kb in final:
                group = slot * BLOCKS + (BLOCKS - 1 - kb)
                keys_here = slice(kb * BQ, kb * BQ + BQ)
                pair = jnp.concatenate(
                    [dk_ref[keys_here, :] * score_scale, dv_ref[keys_here, :]], axis=1
                )
                kv_ref[slot, kb, tensor_of(0, 0)] = pair.T.astype(bf16)
                for copy in own_copies(group):
                    copy.start()
            for stage, ready in DURING.get(group, ()):
                (stage_forward if stage == 0 else stage_far)(ready)

    kept_copy().start()
    for j in range(1, NX):
        count_x(j).wait()
    plane_ref[...] = count_ref[...] + cx_ref[0] + cx_ref[1] + cx_ref[2]
    for j in range(1, NZ):
        count_z(j).start()
    x_copy.wait()
    groups = ROWS * BLOCKS

    def block_of(i):
        shift = jnp.where(i < 2, 0, jnp.where(i < 4, 1, jnp.where(i < 6, 3, 2)))
        return (y + shift) % NY * 2 + (c + i) % 2

    def s1_copy(i, way):
        return remote(
            s1_ref.at[i, way], r1_ref.at[i, way], s1_send.at[i, way], s1_recv.at[i, way],
            at(dx=1 if way == 0 else -1),
        )

    def s2_copy(i, way):
        return remote(
            s2_ref.at[i, way], r2_ref.at[i, way], s2_send.at[i, way], s2_recv.at[i, way],
            at(dx=1 if way == 0 else -1),
        )

    def z_copy(i):
        block = block_of(i)
        return remote(
            zs_ref.at[i], zr_ref.at[z], z_send.at[i], z_recv.at[z], (block * NX + x, lane)
        )

    def part(i, dx, first=0, size=PART):
        begin = pl.multiple_of((x + dx) % NX * PART + first, HALF)
        return wt_ref[i, pl.ds(begin, size), :]

    first_row, second_row = order_ref[0, 0], order_ref[0, 1]

    def own_part(step):
        i = jnp.where(step < 2, step, step - 1)
        return i, (step >= 0) & (i < NT) & (step != 2)

    def gathered(slot, block):
        return jnp.concatenate([kv_ref[slot, kb, block] for kb in range(BLOCKS)], axis=1)

    def wait_group(index, block, half=None):
        @pl.loop(0, groups)
        def _(group):
            kv_copy(group, index, block, half, other).wait_recv()

    @pl.loop(0, NT + 1 + LAG_C)
    def _(step):
        i_a, go_a = own_part(step)

        @pl.when(go_a)
        def _():
            block = block_of(i_a)
            wt_ref[i_a] = jnp.dot(
                gathered(0, block), x_ref[first_row], preferred_element_type=f32
            ) + jnp.dot(gathered(1, block), x_ref[second_row], preferred_element_type=f32)
            s1_ref[i_a, 0] = part(i_a, 2, 0, HALF).astype(bf16)
            s1_ref[i_a, 1] = part(i_a, 2, HALF, HALF).astype(bf16)
            s1_copy(i_a, 0).start()
            s1_copy(i_a, 1).start()

        i_b, go_b = own_part(step - LAG_B)

        @pl.when(go_b)
        def _():
            i = i_b
            s1_copy(i, 0).wait_recv()
            s1_copy(i, 1).wait_recv()
            s2_ref[i, 0, :HALF] = (part(i, 1, 0, HALF) + r1_ref[i, 0].astype(f32)).astype(bf16)
            s2_ref[i, 0, HALF:] = part(i, 1, HALF, HALF).astype(bf16)
            s2_ref[i, 1, :HALF] = part(i, -1, 0, HALF).astype(bf16)
            s2_ref[i, 1, HALF:] = (part(i, -1, HALF, HALF) + r1_ref[i, 1].astype(f32)).astype(bf16)
            s2_copy(i, 0).start()
            s2_copy(i, 1).start()

        i_c, go_c = own_part(step - LAG_C)

        @pl.when(go_c)
        def _():
            i = i_c
            s2_copy(i, 0).wait_recv()
            s2_copy(i, 1).wait_recv()
            reduced = part(i, 0) + r2_ref[i, 0].astype(f32) + r2_ref[i, 1].astype(f32)

            @pl.when(block_of(i) == z)
            def _():
                w_ref[...] = reduced

            @pl.when(block_of(i) != z)
            def _():
                zs_ref[i] = reduced.astype(bf16)
                z_copy(i).start()

        @pl.when(step == 0)
        def _():
            stage_forward(5)
            wait_group(0, tensor_of(0, 1))

        @pl.when(step == 1)
        def _():
            stage_forward(6)

        @pl.when(step == 2)
        def _():
            stage_forward(7)

        @pl.when(step == 3)
        def _():
            wait_group(6, tensor_of(1, 1))

        @pl.when(step == 4)
        def _():
            @pl.loop(0, 5)
            def _(group):
                stage_far(group)

        @pl.when(step == 5)
        def _():
            @pl.loop(5, groups)
            def _(group):
                stage_far(group)

            wait_group(5, tensor_of(-1, 1))

        @pl.when(step == 7)
        def _():
            wait_group(7, tensor_of(2, 1), 0)
            wait_group(8, tensor_of(2, 1), 1)

    total = plane_ref[...]
    for j in range(1, NZ):
        count_z(j).wait()
    for j in range(1, NZ):
        total = total + cz_ref[j - 1]
    scale = loss_scale / total[0:1, 0:1]

    @pl.loop(1, NZ)
    def _(j):
        source = (z + j) % NZ
        remote(
            zs_ref.at[0], zr_ref.at[source], z_send.at[0], z_recv.at[source], at(dz=j)
        ).wait_recv()
        w_ref[...] += zr_ref[source].astype(f32)

    w_ref[...] = w_ref[...] * scale

    @pl.loop(0, NT)
    def _(i):
        for way in range(2):
            s1_copy(i, way).wait_send()
            s2_copy(i, way).wait_send()

        @pl.when(block_of(i) != z)
        def _():
            z_copy(i).wait_send()

    @pl.loop(0, groups)
    def _(group):
        for copy in own_copies(group) + forward_copies(group) + far_copies(group):
            copy.wait_send()

    kept_copy().wait()

    @pl.loop(0, GROUP)
    def _(head):
        for qb in range(BLOCKS):
            dq_copy(qb, head).wait()


def shards(
    layer_input, query_states, key_states, value_states, output_grad, doc_lengths, send_order
):
    def by_rows(array_in):
        return array_in.reshape(ROWS, ROW_LEN, array_in.shape[-1])

    anywhere = pl.BlockSpec(memory_space=pl.ANY)
    scalars = pl.BlockSpec(memory_space=pltpu.SMEM)
    dma = pltpu.SemaphoreType.DMA
    query_grad, weight_grad = pl.pallas_call(
        whole_kernel,
        out_shape=(
            jax.ShapeDtypeStruct((ROWS, ROW_LEN, WIDTH), bf16),
            jax.ShapeDtypeStruct((PART, WIDTH), f32),
        ),
        in_specs=[scalars, scalars] + [anywhere] * 5,
        out_specs=[anywhere, pl.BlockSpec(memory_space=pltpu.VMEM)],
        scratch_shapes=[
            pltpu.VMEM((ROWS, ROW_LEN, WIDTH), bf16),
            pltpu.VMEM((ROWS, ROW_LEN, WIDTH), bf16),
            pltpu.VMEM((ROWS, ROW_LEN, HD), bf16),
            pltpu.VMEM((ROWS, ROW_LEN, HD), bf16),
            pltpu.VMEM((ROWS, ROW_LEN, WIDTH), bf16),
            pltpu.VMEM((HD, ROW_LEN), bf16),
            pltpu.VMEM((ROW_LEN, HD), f32),
            pltpu.VMEM((ROW_LEN, HD), f32),
            pltpu.VMEM((ROWS, ROW_LEN, WIDTH), bf16),
            pltpu.VMEM((ROWS, BLOCKS, NT, FEATURES, BQ), bf16),
            pltpu.VMEM((NT, FEATURES, WIDTH), f32),
            pltpu.VMEM((NT, 2, HALF, WIDTH), bf16),
            pltpu.VMEM((NT, 2, HALF, WIDTH), bf16),
            pltpu.VMEM((NT, 2, PART, WIDTH), bf16),
            pltpu.VMEM((NT, 2, PART, WIDTH), bf16),
            pltpu.VMEM((NT, PART, WIDTH), bf16),
            pltpu.VMEM((NZ, PART, WIDTH), bf16),
            pltpu.VMEM((8, 128), f32),
            pltpu.VMEM((NX - 1, 8, 128), f32),
            pltpu.VMEM((8, 128), f32),
            pltpu.VMEM((NZ - 1, 8, 128), f32),
            dma((3,)),
            dma((2, GROUP)),
            dma((1,)),
            dma((GROUP * BLOCKS,)),
            dma((GROUP * BLOCKS,)),
            dma((ROWS * BLOCKS, 9)),
            dma((ROWS * BLOCKS, 9)),
            dma((NT, 2)),
            dma((NT, 2)),
            dma((NT, 2)),
            dma((NT, 2)),
            dma((NT,)),
            dma((NZ,)),
            dma((NX - 1,)),
            dma((NX - 1,)),
            dma((NZ - 1,)),
            dma((NZ - 1,)),
        ],
        compiler_params=pltpu.CompilerParams(
            collective_id=0, has_side_effects=True, vmem_limit_bytes=60 << 20
        ),
        name="attention_backward_and_weight_grad",
    )(
        send_order,
        doc_lengths,
        by_rows(layer_input),
        by_rows(query_states),
        by_rows(key_states),
        by_rows(value_states),
        by_rows(output_grad),
    )
    return (query_grad.reshape(-1, WIDTH), weight_grad)


def solution(mesh):
    placed = (P("dp", "tensor"),) * 5 + (P("dp", None),) * 2
    return jax.shard_map(
        shards,
        mesh=mesh,
        in_specs=placed,
        out_specs=(P("dp", "tensor"), P("dp", "tensor")),
        check_vma=False,
    )
```
